1024 devices in a mesh: row: 16 (over x, core), col: 64 (over y, z).
Axes of the slice: x: 8, y: 8, z: 8, core: 2. Of those that a mesh axis runs over, the one named last changes fastest.
Arguments:
- inputs: bfloat16 [2048, 6144], P(('row', 'col')), may hold values from -6 to 6
- cotangent: bfloat16 [2048, 6144], P(('row', 'col')), may hold values from -0.41992188 to 0.41992188
- w_in: bfloat16 [1536, 24576], P('row', 'col'), may hold values from -0.15625 to 0.15625
- w_out: bfloat16 [1536, 24576], P('row', 'col'), may hold values from -0.078125 to 0.078125
- keep_in: int32 [192, 12], replicated, may hold values from 0 to 47, all different within a row
- keep_out: int32 [192, 12], replicated, may hold values from 0 to 47, all different within a row
Outputs:
- grad_in: bfloat16 [1536, 24576], P('row', 'col')
- grad_out: bfloat16 [1536, 24576], P('row', 'col')
The draws below stay inside these ranges and needn't reach their ends.
Inputs may be any that keep to these rules, and one draw needn't show every extreme that they name: `keep_in`: each row names 12 different input blocks, and every block is named by some row. `keep_out`: each row names 12 different output blocks, and every block is named by some row.
All inputs are finite; a program needn't handle non-finite values.
Results may differ from the reference program's by a relative error of at most 0.022.
Values may be sent and summed in bfloat16 or wider, within the bound.
A program may use at most 32 MiB of HBM per device.

```python
import jax
import jax.numpy as jnp
from jax import lax

D = 6144
FF = 24576
BLK = 128
TOK = 128
KEEP = 12
TOKENS = 2048
NBF = 192


def steps_of(rng, shape, split, smallest, top_value):
    gain = 1.0
    for axis_at, blocks in split:
        draws = jax.random.uniform(jax.random.fold_in(jax.random.fold_in(rng, 6), axis_at), (blocks,), jnp.float32, smallest / len(split), top_value / len(split))
        gain = gain * jnp.repeat(jnp.exp(draws), shape[axis_at] // blocks).reshape((-1,) + (1,) * (len(shape) - 1 - axis_at))
    return gain


def choose_distinct(stream_key, rows, count, top, lift):
    ranking = jax.random.permutation(jax.random.fold_in(stream_key, 1), count)
    favour = ranking
    for power in range(3):
        favour = favour * favour // count
    favour = favour * lift // count
    lots = jax.random.randint(jax.random.fold_in(stream_key, 2), (rows, count), 0, 4096) + favour
    holders = jax.random.permutation(jax.random.fold_in(stream_key, 3), rows)[jnp.arange(count) % rows]
    lots = jnp.where(jnp.arange(rows)[:, None] == holders[None, :], 1 << 14, lots)
    priority = lots * count + jnp.arange(count)
    return lax.top_k(priority.astype(jnp.int32), top)[1].astype(jnp.int32)


def bell_draw(rng, dims, scale, limit, cuts=(), kind=jnp.bfloat16):
    entries = scale * jax.random.normal(rng, dims, jnp.float32)
    if cuts:
        entries = entries * steps_of(rng, dims, cuts, -0.22, 0.18)
    return jnp.clip(entries, -limit, limit).astype(kind)


def setup_inputs(seed: int = 0) -> dict:
    keys = jax.random.split(jax.random.key(seed), 7)
    inputs = bell_draw(keys[0], (TOKENS, D), 1.0, 6.0, ((0, 1024),))
    cotangent = bell_draw(keys[1], (TOKENS, D), 0.07, 0.41992188, ((0, 1024),))
    w_in = bell_draw(keys[2], (KEEP * BLK, FF), (D // 4) ** -0.5, 0.15625, ((0, 16), (1, 64)))
    w_out = bell_draw(keys[3], (KEEP * BLK, FF), (FF // 4) ** -0.5, 0.078125, ((0, 16), (1, 64)))
    keep_in = choose_distinct(keys[4], NBF, D // BLK, KEEP, 0)
    keep_out = choose_distinct(keys[5], NBF, D // BLK, KEEP, 0)
    return {"inputs": inputs, "cotangent": cotangent, "w_in": w_in, "w_out": w_out, "keep_in": keep_in, "keep_out": keep_out}


def gelu_tanh(values):
    return jax.nn.gelu(values, approximate=True)

def select_blocks(matrix, chosen):
    rows = matrix.shape[0]
    blocks = matrix.reshape(rows, D // BLK, BLK)
    return jnp.take(blocks, chosen, axis=1).reshape(rows, KEEP * BLK)

def group_sum(left, right):
    groups = TOKENS // TOK
    terms = jnp.einsum('gts,gtq->gsq', left.reshape(groups, TOK, KEEP * BLK).astype(jnp.float32), right.reshape(groups, TOK, BLK).astype(jnp.float32))
    rounded = lax.optimization_barrier(terms.astype(jnp.bfloat16))
    return lax.optimization_barrier(jnp.sum(rounded.astype(jnp.float32), axis=0)).astype(jnp.bfloat16)

def reference(inputs, cotangent, w_in, w_out, keep_in, keep_out):

    def one_block(index):
        picked_in = select_blocks(inputs, keep_in[index])
        picked_out = select_blocks(cotangent, keep_out[index])
        panel_in = lax.dynamic_slice_in_dim(w_in, index * BLK, BLK, 1)
        panel_out = lax.dynamic_slice_in_dim(w_out, index * BLK, BLK, 1)
        hidden = jnp.dot(picked_in, panel_in, preferred_element_type=jnp.float32)
        d_act = jnp.dot(picked_out, panel_out, preferred_element_type=jnp.float32)
        act, pullback = jax.vjp(gelu_tanh, hidden)
        d_hidden = pullback(d_act)[0].astype(jnp.bfloat16)
        act = act.astype(jnp.bfloat16)
        return (group_sum(picked_in, d_hidden), group_sum(picked_out, act))
    grad_in, grad_out = lax.map(one_block, jnp.arange(FF // BLK, dtype=jnp.int32))
    grad_in = jnp.transpose(grad_in, (1, 0, 2)).reshape(KEEP * BLK, FF)
    grad_out = jnp.transpose(grad_out, (1, 0, 2)).reshape(KEEP * BLK, FF)
    return (grad_in, grad_out)
```

```python
import functools
import math

import jax
import jax.numpy as jnp
from jax import lax
from jax.experimental import pallas as pl
from jax.experimental.pallas import tpu as pltpu
from jax.sharding import PartitionSpec as P

BLK = 128
MESH = pl.DeviceIdType.MESH
RIGHT, LEFT = 0, 1
SIGN = (1, -1)
FAN = 2


def gelu_terms(hidden):
    scale = math.sqrt(2.0 / math.pi)
    square = hidden * hidden
    curve = jnp.tanh(scale * (hidden + 0.044715 * (square * hidden)))
    half = 0.5 * (1.0 + curve)
    slope = half + 0.5 * hidden * (1.0 - curve * curve) * (scale * (1.0 + 3 * 0.044715 * square))
    return hidden * half, slope


def body(
    nx,
    n,
    x_hbm,
    c_hbm,
    wi_hbm,
    wo_hbm,
    keep_in,
    keep_out,
    gi_ref,
    go_ref,
    gat,
    t32,
    tok_in,
    tok_out,
    wts,
    picked,
    grads,
    sib,
    part,
    land,
    dh,
    act,
    local_sem,
    p1_send,
    p1_recv,
    ring_send,
    ring_recv,
    pair_send,
    pair_recv,
    sib_send,
    sib_recv,
    sum_send,
    sum_recv,
):
    row, col = lax.axis_index("row"), lax.axis_index("col")
    x, core = row // 2, lax.rem(row, 2)
    y, z = col // n, lax.rem(col, n)
    kept, width = wi_hbm.shape
    nb = width // BLK
    tok = (tok_in, tok_out)
    blocks, per_tile, _ = tok_in[0].shape
    tokens = n * per_tile
    half_blocks = blocks // FAN
    keeps = (keep_in, keep_out)
    sibling = (2 * x + 1 - core, col)
    hx, hn = nx // 2, n // 2

    def wrap(at, by, size):
        return lax.rem(at + by % size, size)

    def z_peer(d):
        return (row, y * n + wrap(z, d, n))

    def y_peer(d):
        return (row, wrap(y, d, n) * n + z)

    def x_peer(d):
        return (2 * wrap(x, d, nx) + core, col)

    peers = [z_peer(d) for d in range(1, n)] + [y_peer(d) for d in range(1, n)]
    peers += [x_peer(d) for d in sorted({1, nx - 1})] + [sibling]

    barrier = pltpu.get_barrier_semaphore()
    for peer in peers:
        pl.semaphore_signal(barrier, inc=1, device_id=peer, device_id_type=MESH)
    pl.semaphore_wait(barrier, len(peers))

    sends = []

    def send(src, dst, s_sem, r_sem, device):
        copy = pltpu.make_async_remote_copy(
            src_ref=src, dst_ref=dst, send_sem=s_sem, recv_sem=r_sem, device_id=device, device_id_type=MESH
        )
        copy.start()
        sends.append(copy)

    def arrived(ref, r_sem, s_sem):
        pltpu.make_async_remote_copy(
            src_ref=ref, dst_ref=ref, send_sem=s_sem, recv_sem=r_sem, device_id=sibling, device_id_type=MESH
        ).wait_recv()

    ring_size = (n, n, nx)
    ring_peer = (y_peer, z_peer, x_peer)

    def weight_rows(dist, whose):
        start = pl.multiple_of((2 * wrap(x, dist, nx) + whose) * kept, kept)
        return pl.ds(start, kept)

    def piece(ring, dist, part_at):
        if ring == 2:
            return wts.at[part_at, weight_rows(dist, core), :]
        return tok[ring][dist % n].at[pl.ds(part_at * half_blocks, half_blocks)]

    def ring_start(ring, way, step, part_at, src=None):
        ref = piece(ring, -(step - 1) * SIGN[way], part_at)
        send(
            ref if src is None else src,
            ref if ring == 2 else piece(ring, -step * SIGN[way], part_at),
            ring_send.at[ring, way, step - 1, part_at],
            ring_recv.at[ring, way, step - 1, part_at],
            ring_peer[ring](SIGN[way]),
        )

    def ring_takes(ring, way, step, part_at):
        top = ring_size[ring] // 2
        return step < top or (step == top and part_at == way)

    def pair_start(dist_at, dist, part_at, src=None):
        ref = wts.at[part_at, weight_rows(dist, core), :]
        send(
            ref if src is None else src,
            ref,
            pair_send.at[dist_at, part_at],
            pair_recv.at[dist_at, part_at],
            sibling,
        )

    def place(array, dist):
        first = col * nb
        at = slice(dist % n * per_tile, (dist % n + 1) * per_tile)

        def one(c, carry):
            for s in range(keep_in.shape[1]):
                block = keeps[array][first + c, s]
                picked[array, c, at, s * BLK : (s + 1) * BLK] = tok[array][dist % n][block]
            return carry

        lax.fori_loop(0, nb, one, 0)

    local = [
        pltpu.make_async_copy(x_hbm, gat.at[0, 0], local_sem.at[0]),
        pltpu.make_async_copy(c_hbm, gat.at[1, 0], local_sem.at[1]),
        pltpu.make_async_copy(wi_hbm, wts.at[0, weight_rows(0, core), :], local_sem.at[2]),
        pltpu.make_async_copy(wo_hbm, wts.at[1, weight_rows(0, core), :], local_sem.at[3]),
    ]
    for copy in local:
        copy.start()
    order = sorted(range(1, n), key=lambda d: -min(d, n - d))
    for d in order:
        for array, (src, peer) in enumerate(((x_hbm, z_peer), (c_hbm, y_peer))):
            send(src, gat.at[array, n - d], p1_send.at[array, d], p1_recv.at[array, n - d], peer(d))
    for part_at, src in enumerate((wi_hbm, wo_hbm)):
        for way in (RIGHT, LEFT):
            if ring_takes(2, way, 1, part_at):
                ring_start(2, way, 1, part_at, src)
        pair_start(0, 0, part_at, src)

    for array in (0, 1):
        for d in [0] + order[::-1]:
            if d == 0:
                local[array].wait()
            else:
                arrived(gat.at[array, d], p1_recv.at[array, d], p1_send.at[array, d])
            t32[array, 2 * d : 2 * d + 2, :] = gat[array, d].astype(jnp.float32)
        for b in range(blocks):
            tok[array][0][b] = t32[array, :, b * BLK : (b + 1) * BLK].astype(jnp.bfloat16)
        for part_at in range(FAN):
            for way in (RIGHT, LEFT):
                if ring_takes(array, way, 1, part_at):
                    ring_start(array, way, 1, part_at)
    for array in (0, 1):
        place(array, 0)

    for step in range(1, max(hx, hn) + 1):
        for part_at in range(FAN):
            for ring in (2, 0, 1):
                for way in (RIGHT, LEFT):
                    if not ring_takes(ring, way, step, part_at):
                        continue
                    dist = -step * SIGN[way]
                    ref = piece(ring, dist, part_at)
                    arrived(ref, ring_recv.at[ring, way, step - 1, part_at], ring_send.at[ring, way, step - 1, part_at])
                    if ring_takes(ring, way, step + 1, part_at):
                        ring_start(ring, way, step + 1, part_at)
                    if ring == 2:
                        pair_start(step + way * hx, dist, part_at)
        for array in (0, 1):
            if step < hn:
                place(array, step)
                place(array, -step)
            elif step == hn:
                place(array, step)

    def pair_dists():
        for part_at in range(FAN):
            yield 0, 0, part_at
            for step in range(1, hx + 1):
                for way in (RIGHT, LEFT):
                    if ring_takes(2, way, step, part_at):
                        yield step + way * hx, -step * SIGN[way], part_at

    for dist_at, dist, part_at in pair_dists():
        arrived(
            wts.at[part_at, weight_rows(dist, 1 - core), :],
            pair_recv.at[dist_at, part_at],
            pair_send.at[dist_at, part_at],
        )
    local[2].wait()
    local[3].wait()

    r_at = lax.broadcasted_iota(jnp.int32, (tokens, tokens), 0)
    c_at = lax.broadcasted_iota(jnp.int32, (tokens, tokens), 1)
    r_y, r_z = r_at // per_tile, lax.rem(r_at, per_tile) // 2
    c_z, c_y = c_at // per_tile, lax.rem(c_at, per_tile) // 2
    same = (r_y == c_y) & (r_z == c_z) & (lax.rem(r_at, 2) == lax.rem(c_at, 2))
    swap = jnp.where(same, 1.0, 0.0)
    swap_half = swap.astype(jnp.bfloat16)
    across = (((0,), (0,)), ((), ()))
    for c in range(nb):
        lanes = slice(c * BLK, (c + 1) * BLK)
        hidden = jnp.dot(picked[0, c], wts[0, :, lanes], preferred_element_type=jnp.float32)
        d_act = jnp.dot(picked[1, c], wts[1, :, lanes], preferred_element_type=jnp.float32)
        d_act = jnp.dot(swap, d_act, preferred_element_type=jnp.float32, precision=lax.Precision.HIGHEST)
        value, slope = gelu_terms(hidden)
        dh[:, lanes] = (d_act * slope).astype(jnp.bfloat16)
        act[:, lanes] = lax.dot_general(
            swap_half, value.astype(jnp.bfloat16), across, preferred_element_type=jnp.float32
        ).astype(jnp.bfloat16)
    for c in range(nb):
        lanes = slice(c * BLK, (c + 1) * BLK)
        for array, right in enumerate((dh, act)):
            grads[array, :, lanes] = lax.dot_general(
                picked[array, c], right[:, lanes], across, preferred_element_type=jnp.float32
            ).astype(jnp.bfloat16)

    offsets = [hx] + [sign * d for d in range(hx - 1, 0, -1) for sign in SIGN] + [0]

    for at, dist in enumerate(offsets):
        send(
            grads.at[:, weight_rows(dist, 1 - core), :],
            sib.at[at],
            sib_send.at[at],
            sib_recv.at[at],
            sibling,
        )

    slot_of = {dist: at for at, dist in enumerate(offsets)}
    slot_of[-hx] = slot_of[hx]

    def sum_start(way, dist, array):
        src = part.at[slot_of[dist * SIGN[way]], array]
        send(
            src,
            land.at[way, dist - 1, array],
            sum_send.at[way, dist - 1, array],
            sum_recv.at[way, dist - 1, array],
            x_peer(SIGN[way]),
        )

    def first_hop(way, array):
        return hx if array == way else hx - 1

    for at, dist in enumerate(offsets):
        arrived(sib.at[at], sib_recv.at[at], sib_send.at[at])
        for array in (0, 1):
            own = grads[array, weight_rows(dist, core), :].astype(jnp.float32)
            part[at, array] = (own + sib[at, array].astype(jnp.float32)).astype(jnp.bfloat16)
        for array in (0, 1):
            for way in (RIGHT, LEFT):
                far = first_hop(way, array)
                if far >= 1 and (dist == far * SIGN[way] or (far == hx and dist == hx)):
                    sum_start(way, far, array)

    for dist in range(hx - 1, 0, -1):
        for which in (0, 1):
            for way in (RIGHT, LEFT):
                array = which ^ way
                if dist + 1 > first_hop(way, array):
                    continue
                ref = land.at[way, dist, array]
                arrived(ref, sum_recv.at[way, dist, array], sum_send.at[way, dist, array])
                at = slot_of[dist * SIGN[way]]
                total = part[at, array].astype(jnp.float32) + land[way, dist, array].astype(jnp.float32)
                part[at, array] = total.astype(jnp.bfloat16)
                sum_start(way, dist, array)

    for array, out in enumerate((gi_ref, go_ref)):
        total = part[slot_of[0], array].astype(jnp.float32)
        for way in (RIGHT, LEFT):
            if first_hop(way, array) >= 1:
                ref = land.at[way, 0, array]
                arrived(ref, sum_recv.at[way, 0, array], sum_send.at[way, 0, array])
                total = total + land[way, 0, array].astype(jnp.float32)
        out[...] = total.astype(jnp.bfloat16)

    for copy in sends:
        copy.wait_send()


def per_device(inputs, cotangent, w_in, w_out, keep_in, keep_out):
    nx = lax.axis_size("row") // 2
    n = math.isqrt(lax.axis_size("col"))
    features = inputs.shape[1]
    kept, width = w_in.shape
    rows = 2 * nx * kept
    nb = width // BLK
    per_tile = 2 * n
    tokens = n * per_tile
    half = jnp.bfloat16
    any_spec = pl.BlockSpec(memory_space=pl.ANY)
    smem_spec = pl.BlockSpec(memory_space=pltpu.SMEM)
    vmem_spec = pl.BlockSpec(memory_space=pltpu.VMEM)
    dma = pltpu.SemaphoreType.DMA
    top = max(nx, n) // 2
    return pl.pallas_call(
        functools.partial(body, nx, n),
        out_shape=(jax.ShapeDtypeStruct((kept, width), half),) * 2,
        in_specs=[any_spec] * 4 + [smem_spec] * 2,
        out_specs=(vmem_spec, vmem_spec),
        scratch_shapes=[
            pltpu.VMEM((2, n, 2, features), half),
            pltpu.VMEM((2, per_tile, features), jnp.float32),
            [pltpu.VMEM((features // BLK, per_tile, BLK), half)] * n,
            [pltpu.VMEM((features // BLK, per_tile, BLK), half)] * n,
            pltpu.VMEM((2, rows, width), half),
            pltpu.VMEM((2, nb, tokens, rows), half),
            pltpu.VMEM((2, rows, width), half),
            pltpu.VMEM((nx, 2, kept, width), half),
            pltpu.VMEM((nx, 2, kept, width), half),
            pltpu.VMEM((2, nx // 2, 2, kept, width), half),
            pltpu.VMEM((tokens, width), half),
            pltpu.VMEM((tokens, width), half),
            dma((4,)),
            dma((2, n)),
            dma((2, n)),
            dma((3, 2, top, FAN)),
            dma((3, 2, top, FAN)),
            dma((nx + 1, FAN)),
            dma((nx + 1, FAN)),
            dma((nx,)),
            dma((nx,)),
            dma((2, nx // 2, 2)),
            dma((2, nx // 2, 2)),
        ],
        compiler_params=pltpu.CompilerParams(
            collective_id=0, has_side_effects=True, vmem_limit_bytes=48 * 1024 * 1024
        ),
        name="mlp_backward",
    )(inputs, cotangent, w_in, w_out, keep_in, keep_out)


def solution(mesh):
    in_specs = (
        P(("row", "col"), None),
        P(("row", "col"), None),
        P("row", "col"),
        P("row", "col"),
        P(),
        P(),
    )
    out_specs = (P("row", "col"), P("row", "col"))
    return jax.shard_map(
        per_device, mesh=mesh, in_specs=in_specs, out_specs=out_specs, check_vma=False
    )
```

```python
import functools
import math

import jax
import jax.numpy as jnp
from jax import lax
from jax.experimental import pallas as pl
from jax.experimental.pallas import tpu as pltpu
from jax.sharding import PartitionSpec as P

BLK = 128
MESH = pl.DeviceIdType.MESH
RIGHT, LEFT = 0, 1
SIGN = (1, -1)
FAN = 4
HALVES = 2
ROW_PARTS = 2


def gelu_terms(hidden):
    scale = math.sqrt(2.0 / math.pi)
    square = hidden * hidden
    curve = jnp.tanh(scale * (hidden + 0.044715 * (square * hidden)))
    half = 0.5 * (1.0 + curve)
    slope = half + 0.5 * hidden * (1.0 - curve * curve) * (scale * (1.0 + 3 * 0.044715 * square))
    return hidden * half, slope


def body(
    nx,
    n,
    x_hbm,
    c_hbm,
    wi_hbm,
    wo_hbm,
    keep_in_hbm,
    keep_out_hbm,
    gi_ref,
    go_ref,
    gat,
    t32,
    tok_in,
    tok_out,
    wts,
    picked,
    grads,
    sib,
    part,
    land,
    dh,
    act,
    keep_in,
    keep_out,
    local_sem,
    p1_send,
    p1_recv,
    ring_send,
    ring_recv,
    pair_send,
    pair_recv,
    sib_send,
    sib_recv,
    sum_send,
    sum_recv,
):
    row, col = lax.axis_index("row"), lax.axis_index("col")
    x, core = row // 2, lax.rem(row, 2)
    y, z = col // n, lax.rem(col, n)
    kept, width = wi_hbm.shape
    nb = width // BLK
    tok = (tok_in, tok_out)
    blocks, per_tile, _ = tok_in[0].shape
    tokens = n * per_tile
    fan_blocks = blocks // FAN
    half_blocks = blocks // HALVES
    keeps = (keep_in, keep_out)
    sibling = (2 * x + 1 - core, col)
    hx, hn = nx // 2, n // 2

    def wrap(at, by, size):
        return lax.rem(at + by % size, size)

    def z_peer(d):
        return (row, y * n + wrap(z, d, n))

    def y_peer(d):
        return (row, wrap(y, d, n) * n + z)

    def x_peer(d):
        return (2 * wrap(x, d, nx) + core, col)

    peers = [z_peer(d) for d in range(1, n)] + [y_peer(d) for d in range(1, n)]
    peers += [x_peer(d) for d in sorted({1, nx - 1})] + [sibling]

    def weight_rows(dist, whose):
        start = pl.multiple_of((2 * wrap(x, dist, nx) + whose) * kept, kept)
        return pl.ds(start, kept)

    def half_lanes(half):
        return pl.ds(half * half_blocks * BLK, half_blocks * BLK)

    local = [
        pltpu.make_async_copy(src.at[:, half_lanes(half)], gat.at[array, half, 0], local_sem.at[array, half])
        for array, src in enumerate((x_hbm, c_hbm))
        for half in range(HALVES)
    ]
    local += [
        pltpu.make_async_copy(wi_hbm, wts.at[0, weight_rows(0, core), :], local_sem.at[2, 0]),
        pltpu.make_async_copy(wo_hbm, wts.at[1, weight_rows(0, core), :], local_sem.at[2, 1]),
        pltpu.make_async_copy(keep_in_hbm, keep_in, local_sem.at[3, 0]),
        pltpu.make_async_copy(keep_out_hbm, keep_out, local_sem.at[3, 1]),
    ]
    for copy in local:
        copy.start()

    barrier = pltpu.get_barrier_semaphore()
    for peer in peers:
        pl.semaphore_signal(barrier, inc=1, device_id=peer, device_id_type=MESH)
    pl.semaphore_wait(barrier, len(peers))

    sends = []

    def send(src, dst, s_sem, r_sem, device):
        copy = pltpu.make_async_remote_copy(
            src_ref=src, dst_ref=dst, send_sem=s_sem, recv_sem=r_sem, device_id=device, device_id_type=MESH
        )
        copy.start()
        sends.append(copy)

    def arrived(ref, r_sem, s_sem):
        pltpu.make_async_remote_copy(
            src_ref=ref, dst_ref=ref, send_sem=s_sem, recv_sem=r_sem, device_id=sibling, device_id_type=MESH
        ).wait_recv()

    ring_size = (n, n, nx)
    fans = (FAN, FAN, 2)
    ring_peer = (y_peer, z_peer, x_peer)

    def piece(ring, dist, part_at):
        if ring == 2:
            return wts.at[part_at, weight_rows(dist, core), :]
        return tok[ring][dist % n].at[pl.ds(part_at * fan_blocks, fan_blocks)]

    def ring_start(ring, way, step, part_at, src=None):
        ref = piece(ring, -(step - 1) * SIGN[way], part_at)
        send(
            ref if src is None else src,
            ref if ring == 2 else piece(ring, -step * SIGN[way], part_at),
            ring_send.at[ring, way, step - 1, part_at],
            ring_recv.at[ring, way, step - 1, part_at],
            ring_peer[ring](SIGN[way]),
        )

    def ring_takes(ring, way, step, part_at):
        top = ring_size[ring] // 2
        return step < top or (step == top and part_at * 2 // fans[ring] == way)

    def pair_start(dist_at, dist, part_at, src=None):
        ref = wts.at[part_at, weight_rows(dist, core), :]
        send(
            ref if src is None else src,
            ref,
            pair_send.at[dist_at, part_at],
            pair_recv.at[dist_at, part_at],
            sibling,
        )

    def place(array, dist):
        first = col * nb
        at = slice(dist % n * per_tile, (dist % n + 1) * per_tile)

        def one(c, carry):
            for s in range(keep_in.shape[0]):
                block = keeps[array][s, first + c]
                picked[array, c, at, s * BLK : (s + 1) * BLK] = tok[array][dist % n][block]
            return carry

        lax.fori_loop(0, nb, one, 0)

    order = sorted(range(1, n), key=lambda d: -min(d, n - d))
    for half in range(HALVES):
        for d in order:
            for array, (src, peer) in enumerate(((x_hbm, z_peer), (c_hbm, y_peer))):
                send(
                    src.at[:, half_lanes(half)],
                    gat.at[array, half, n - d],
                    p1_send.at[array, half, d],
                    p1_recv.at[array, half, n - d],
                    peer(d),
                )
    for part_at, src in enumerate((wi_hbm, wo_hbm)):
        for way in (RIGHT, LEFT):
            if ring_takes(2, way, 1, part_at):
                ring_start(2, way, 1, part_at, src)
        pair_start(0, 0, part_at, src)

    for half in range(HALVES):
        for array in (0, 1):
            for d in [0] + order[::-1]:
                if d == 0:
                    local[array * HALVES + half].wait()
                else:
                    arrived(gat.at[array, half, d], p1_recv.at[array, half, d], p1_send.at[array, half, d])
                t32[array, half, 2 * d : 2 * d + 2, :] = gat[array, half, d].astype(jnp.float32)
            for b in range(half_blocks):
                tok[array][0][half * half_blocks + b] = t32[array, half, :, b * BLK : (b + 1) * BLK].astype(jnp.bfloat16)
            for part_at in range(half * FAN // HALVES, (half + 1) * FAN // HALVES):
                for way in (RIGHT, LEFT):
                    if ring_takes(array, way, 1, part_at):
                        ring_start(array, way, 1, part_at)
    for copy in local[-2:]:
        copy.wait()
    for array in (0, 1):
        place(array, 0)

    for step in range(1, max(hx, hn) + 1):
        for part_at in range(FAN):
            for ring in (2, 0, 1):
                for way in (RIGHT, LEFT):
                    if part_at >= fans[ring] or not ring_takes(ring, way, step, part_at):
                        continue
                    dist = -step * SIGN[way]
                    ref = piece(ring, dist, part_at)
                    arrived(ref, ring_recv.at[ring, way, step - 1, part_at], ring_send.at[ring, way, step - 1, part_at])
                    if ring_takes(ring, way, step + 1, part_at):
                        ring_start(ring, way, step + 1, part_at)
                    if ring == 2:
                        pair_start(step + way * hx, dist, part_at)
        for array in (0, 1):
            if step < hn:
                place(array, step)
                place(array, -step)
            elif step == hn:
                place(array, step)

    def pair_dists():
        for part_at in (0, 1):
            yield 0, 0, part_at
            for step in range(1, hx + 1):
                for way in (RIGHT, LEFT):
                    if ring_takes(2, way, step, part_at):
                        yield step + way * hx, -step * SIGN[way], part_at

    for dist_at, dist, part_at in pair_dists():
        arrived(
            wts.at[part_at, weight_rows(dist, 1 - core), :],
            pair_recv.at[dist_at, part_at],
            pair_send.at[dist_at, part_at],
        )
    for copy in local[2 * HALVES : 2 * HALVES + 2]:
        copy.wait()

    r_at = lax.broadcasted_iota(jnp.int32, (tokens, tokens), 0)
    c_at = lax.broadcasted_iota(jnp.int32, (tokens, tokens), 1)
    r_y, r_z = r_at // per_tile, lax.rem(r_at, per_tile) // 2
    c_z, c_y = c_at // per_tile, lax.rem(c_at, per_tile) // 2
    same = (r_y == c_y) & (r_z == c_z) & (lax.rem(r_at, 2) == lax.rem(c_at, 2))
    swap = jnp.where(same, 1.0, 0.0)
    swap_half = swap.astype(jnp.bfloat16)
    across = (((0,), (0,)), ((), ()))
    for c in range(nb):
        lanes = slice(c * BLK, (c + 1) * BLK)
        hidden = jnp.dot(picked[0, c], wts[0, :, lanes], preferred_element_type=jnp.float32)
        d_act = jnp.dot(picked[1, c], wts[1, :, lanes], preferred_element_type=jnp.float32)
        d_act = jnp.dot(swap, d_act, preferred_element_type=jnp.float32, precision=lax.Precision.HIGHEST)
        value, slope = gelu_terms(hidden)
        dh[:, lanes] = (d_act * slope).astype(jnp.bfloat16)
        act[:, lanes] = lax.dot_general(
            swap_half, value.astype(jnp.bfloat16), across, preferred_element_type=jnp.float32
        ).astype(jnp.bfloat16)

    groups = nx // 2
    group_rows = 4 * kept
    odd = lax.rem(x, 2)
    shifts = sorted(range(groups), key=lambda g: (-min(g, groups - g), g))

    def chip_of(shift, member):
        return 2 * lax.rem(x // 2 + shift, groups) + member

    def shard(chip, whose):
        return pl.ds(pl.multiple_of((2 * chip + whose) * kept, kept), kept)

    def group_compute(at):
        start = pl.multiple_of(lax.rem(x // 2 + shifts[at], groups) * group_rows, group_rows)
        for c in range(nb):
            lanes = slice(c * BLK, (c + 1) * BLK)
            for array, right in enumerate((dh, act)):
                grads[array, pl.ds(start, group_rows), lanes] = lax.dot_general(
                    picked[array, c, :, pl.ds(start, group_rows)],
                    right[:, lanes],
                    across,
                    preferred_element_type=jnp.float32,
                ).astype(jnp.bfloat16)
        for member in (0, 1):
            send(
                grads.at[:, shard(chip_of(shifts[at], member), 1 - core), :],
                sib.at[at, member],
                sib_send.at[at, member],
                sib_recv.at[at, member],
                sibling,
            )

    def group_sum(at):
        for member in (0, 1):
            arrived(sib.at[at, member], sib_recv.at[at, member], sib_send.at[at, member])
            to = lax.rem(2 * shifts[at] + member - odd + nx, nx)
            own = shard(chip_of(shifts[at], member), core)
            for array in (0, 1):
                total = grads[array, own, :].astype(jnp.float32) + sib[at, member, array].astype(jnp.float32)
                part[to, array] = total.astype(jnp.bfloat16)

    chunk = kept // ROW_PARTS

    def sum_start(way, dist, array, r):
        rows = pl.ds(r * chunk, chunk)
        send(
            part.at[dist * SIGN[way] % nx, array, rows],
            land.at[way, dist - 1, array, rows],
            sum_send.at[way, dist - 1, array, r],
            sum_recv.at[way, dist - 1, array, r],
            x_peer(SIGN[way]),
        )

    def sum_arrived(way, dist, array, r):
        rows = pl.ds(r * chunk, chunk)
        ref = land.at[way, dist - 1, array, rows]
        arrived(ref, sum_recv.at[way, dist - 1, array, r], sum_send.at[way, dist - 1, array, r])
        return land[way, dist - 1, array, r * chunk : (r + 1) * chunk].astype(jnp.float32)

    def first_hop(way, array):
        return hx if array == way else hx - 1

    group_compute(0)
    if groups > 1:
        group_compute(1)
    group_sum(0)
    for r in range(ROW_PARTS):
        for way in (RIGHT, LEFT):
            sum_start(way, hx, way, r)
    if groups > 1:
        for at in range(2, groups - 1):
            group_compute(at)
        for at in range(1, groups - 1):
            group_sum(at)
        if groups == 2:
            group_sum(1)
        for r in range(ROW_PARTS):
            for way in (RIGHT, LEFT):
                sum_start(way, hx - 1, 1 - way, r)
        if groups > 2:
            group_compute(groups - 1)
            group_sum(groups - 1)

    for dist in range(hx - 1, 0, -1):
        for which in (1, 0):
            for r in range(ROW_PARTS):
                for way in (RIGHT, LEFT):
                    array = which ^ way
                    if dist + 1 > first_hop(way, array):
                        continue
                    came = sum_arrived(way, dist + 1, array, r)
                    at, rows = dist * SIGN[way] % nx, slice(r * chunk, (r + 1) * chunk)
                    part[at, array, rows] = (part[at, array, rows].astype(jnp.float32) + came).astype(jnp.bfloat16)
                    sum_start(way, dist, array, r)

    for array, out in enumerate((gi_ref, go_ref)):
        for r in range(ROW_PARTS):
            rows = slice(r * chunk, (r + 1) * chunk)
            total = part[0, array, rows].astype(jnp.float32)
            for way in (1 - array, array):
                if first_hop(way, array) >= 1:
                    total = total + sum_arrived(way, 1, array, r)
            out[rows, :] = total.astype(jnp.bfloat16)

    for copy in sends:
        copy.wait_send()


def per_device(inputs, cotangent, w_in, w_out, keep_in, keep_out):
    nx = lax.axis_size("row") // 2
    n = math.isqrt(lax.axis_size("col"))
    features = inputs.shape[1]
    kept, width = w_in.shape
    rows = 2 * nx * kept
    nb = width // BLK
    per_tile = 2 * n
    tokens = n * per_tile
    half = jnp.bfloat16
    hbm_spec = pl.BlockSpec(memory_space=pltpu.HBM)
    vmem_spec = pl.BlockSpec(memory_space=pltpu.VMEM)
    dma = pltpu.SemaphoreType.DMA
    top = max(nx, n) // 2
    return pl.pallas_call(
        functools.partial(body, nx, n),
        out_shape=(jax.ShapeDtypeStruct((kept, width), half),) * 2,
        in_specs=[hbm_spec] * 6,
        out_specs=(vmem_spec, vmem_spec),
        scratch_shapes=[
            pltpu.VMEM((2, HALVES, n, 2, features // HALVES), half),
            pltpu.VMEM((2, HALVES, per_tile, features // HALVES), jnp.float32),
            [pltpu.VMEM((features // BLK, per_tile, BLK), half)] * n,
            [pltpu.VMEM((features // BLK, per_tile, BLK), half)] * n,
            pltpu.VMEM((2, rows, width), half),
            pltpu.VMEM((2, nb, tokens, rows), half),
            pltpu.VMEM((2, rows, width), half),
            pltpu.VMEM((nx // 2, 2, 2, kept, width), half),
            pltpu.VMEM((nx, 2, kept, width), half),
            pltpu.VMEM((2, nx // 2, 2, kept, width), half),
            pltpu.VMEM((tokens, width), half),
            pltpu.VMEM((tokens, width), half),
            pltpu.SMEM(keep_in.shape[::-1], jnp.int32),
            pltpu.SMEM(keep_out.shape[::-1], jnp.int32),
            dma((4, 2)),
            dma((2, HALVES, n)),
            dma((2, HALVES, n)),
            dma((3, 2, top, FAN)),
            dma((3, 2, top, FAN)),
            dma((nx + 1, 2)),
            dma((nx + 1, 2)),
            dma((nx // 2, 2)),
            dma((nx // 2, 2)),
            dma((2, nx // 2, 2, ROW_PARTS)),
            dma((2, nx // 2, 2, ROW_PARTS)),
        ],
        compiler_params=pltpu.CompilerParams(
            collective_id=0, has_side_effects=True, vmem_limit_bytes=60 * 1024 * 1024
        ),
        name="mlp_backward",
    )(inputs, cotangent, w_in, w_out, keep_in.T, keep_out.T)


def solution(mesh):
    in_specs = (
        P(("row", "col"), None),
        P(("row", "col"), None),
        P("row", "col"),
        P("row", "col"),
        P(),
        P(),
    )
    out_specs = (P("row", "col"), P("row", "col"))
    return jax.shard_map(
        per_device, mesh=mesh, in_specs=in_specs, out_specs=out_specs, check_vma=False
    )
```

```python
import functools
import math

import jax
import jax.numpy as jnp
from jax import lax
from jax.experimental import pallas as pl
from jax.experimental.pallas import tpu as pltpu
from jax.sharding import PartitionSpec as P

BLK = 128
MESH = pl.DeviceIdType.MESH
RIGHT, LEFT = 0, 1
SIGN = (1, -1)
FAN = 4
TILES = 2
ROW_PARTS = 2


def gelu_terms(hidden):
    scale = math.sqrt(2.0 / math.pi)
    square = hidden * hidden
    curve = jnp.tanh(scale * (hidden + 0.044715 * (square * hidden)))
    half = 0.5 * (1.0 + curve)
    slope = half + 0.5 * hidden * (1.0 - curve * curve) * (scale * (1.0 + 3 * 0.044715 * square))
    return hidden * half, slope


def body(
    nx,
    n,
    x_hbm,
    c_hbm,
    wi_hbm,
    wo_hbm,
    keep_in_hbm,
    keep_out_hbm,
    out_ref,
    gat,
    t32,
    tok_in,
    tok_out,
    wts,
    picked,
    grads,
    sib,
    part,
    land,
    dh,
    act,
    keep_in,
    keep_out,
    local_sem,
    p1_send,
    p1_recv,
    ring_send,
    ring_recv,
    pair_send,
    pair_recv,
    sib_send,
    sib_recv,
    sum_send,
    sum_recv,
):
    row, col = lax.axis_index("row"), lax.axis_index("col")
    x, core = row // 2, lax.rem(row, 2)
    y, z = col // n, lax.rem(col, n)
    kept, width = wi_hbm.shape
    nb = width // BLK
    tok = (tok_in, tok_out)
    _, blocks, per_tile, _ = tok_in[0].shape
    tokens = n * TILES * per_tile
    fan_blocks = blocks * TILES // FAN
    keeps = (keep_in, keep_out)
    sibling = (2 * x + 1 - core, col)
    hx, hn = nx // 2, n // 2

    def wrap(at, by, size):
        return lax.rem(at + by % size, size)

    def z_peer(d):
        return (row, y * n + wrap(z, d, n))

    def y_peer(d):
        return (row, wrap(y, d, n) * n + z)

    def x_peer(d):
        return (2 * wrap(x, d, nx) + core, col)

    peers = [z_peer(d) for d in range(1, n)] + [y_peer(d) for d in range(1, n)]
    peers += [x_peer(d) for d in sorted({1, nx - 1})] + [sibling]

    def weight_rows(dist, whose):
        start = pl.multiple_of((2 * wrap(x, dist, nx) + whose) * kept, kept)
        return pl.ds(start, kept)

    local = [
        pltpu.make_async_copy(src, gat.at[array, 0], local_sem.at[array, 0])
        for array, src in enumerate((x_hbm, c_hbm))
    ]
    local += [
        pltpu.make_async_copy(wi_hbm, wts.at[0, weight_rows(0, core), :], local_sem.at[2, 0]),
        pltpu.make_async_copy(wo_hbm, wts.at[1, weight_rows(0, core), :], local_sem.at[2, 1]),
        pltpu.make_async_copy(keep_in_hbm, keep_in, local_sem.at[3, 0]),
        pltpu.make_async_copy(keep_out_hbm, keep_out, local_sem.at[3, 1]),
    ]
    for copy in local:
        copy.start()

    barrier = pltpu.get_barrier_semaphore()
    for peer in peers:
        pl.semaphore_signal(barrier, inc=1, device_id=peer, device_id_type=MESH)
    pl.semaphore_wait(barrier, len(peers))

    sends = []

    def send(src, dst, s_sem, r_sem, device):
        copy = pltpu.make_async_remote_copy(
            src_ref=src, dst_ref=dst, send_sem=s_sem, recv_sem=r_sem, device_id=device, device_id_type=MESH
        )
        copy.start()
        sends.append(copy)

    def arrived(ref, r_sem, s_sem):
        pltpu.make_async_remote_copy(
            src_ref=ref, dst_ref=ref, send_sem=s_sem, recv_sem=r_sem, device_id=sibling, device_id_type=MESH
        ).wait_recv()

    ring_size = (n, n, nx)
    fans = (FAN, FAN, 2)
    ring_peer = (y_peer, z_peer, x_peer)

    def piece(ring, dist, part_at):
        if ring == 2:
            return wts.at[part_at, weight_rows(dist, core), :]
        tile, cut = divmod(part_at, FAN // TILES)
        return tok[ring][dist % n].at[tile, pl.ds(cut * fan_blocks, fan_blocks)]

    def ring_start(ring, way, step, part_at, src=None):
        ref = piece(ring, -(step - 1) * SIGN[way], part_at)
        send(
            ref if src is None else src,
            ref if ring == 2 else piece(ring, -step * SIGN[way], part_at),
            ring_send.at[ring, way, step - 1, part_at],
            ring_recv.at[ring, way, step - 1, part_at],
            ring_peer[ring](SIGN[way]),
        )

    def ring_takes(ring, way, step, part_at):
        top = ring_size[ring] // 2
        return step < top or (step == top and part_at * 2 // fans[ring] == way)

    def pair_start(dist_at, dist, part_at, src=None):
        ref = wts.at[part_at, weight_rows(dist, core), :]
        send(
            ref if src is None else src,
            ref,
            pair_send.at[dist_at, part_at],
            pair_recv.at[dist_at, part_at],
            sibling,
        )

    def place(array, dist):
        first = col * nb
        top = dist % n * TILES * per_tile

        def one(c, carry):
            for s in range(keep_in.shape[0]):
                block = keeps[array][s, first + c]
                for tile in range(TILES):
                    rows = slice(top + tile * per_tile, top + (tile + 1) * per_tile)
                    picked[array, c, rows, s * BLK : (s + 1) * BLK] = tok[array][dist % n][tile, block]
            return carry

        lax.fori_loop(0, nb, one, 0)

    near = sorted(range(n), key=lambda d: (min(d, n - d), d))
    for d in near[1:]:
        for array, (src, peer) in enumerate(((x_hbm, z_peer), (c_hbm, y_peer))):
            send(src, gat.at[array, d], p1_send.at[array, d], p1_recv.at[array, d], peer(n - d))
    for part_at, src in enumerate((wi_hbm, wo_hbm)):
        for way in (RIGHT, LEFT):
            if ring_takes(2, way, 1, part_at):
                ring_start(2, way, 1, part_at, src)
        pair_start(0, 0, part_at, src)

    for tile in range(TILES):
        for array in (0, 1):
            for at, d in enumerate(near[tile * n // TILES : (tile + 1) * n // TILES]):
                if d == 0:
                    local[array].wait()
                else:
                    arrived(gat.at[array, d], p1_recv.at[array, d], p1_send.at[array, d])
                t32[array, tile, 2 * at : 2 * at + 2, :] = gat[array, d].astype(jnp.float32)
            for b in range(blocks):
                tok[array][0][tile, b] = t32[array, tile, :, b * BLK : (b + 1) * BLK].astype(jnp.bfloat16)
            for part_at in range(tile * FAN // TILES, (tile + 1) * FAN // TILES):
                for way in (RIGHT, LEFT):
                    if ring_takes(array, way, 1, part_at):
                        ring_start(array, way, 1, part_at)
    for copy in local[-2:]:
        copy.wait()
    for array in (0, 1):
        place(array, 0)

    for step in range(1, max(hx, hn) + 1):
        for part_at in range(FAN):
            for ring in (2, 0, 1):
                for way in (RIGHT, LEFT):
                    if part_at >= fans[ring] or not ring_takes(ring, way, step, part_at):
                        continue
                    dist = -step * SIGN[way]
                    ref = piece(ring, dist, part_at)
                    arrived(ref, ring_recv.at[ring, way, step - 1, part_at], ring_send.at[ring, way, step - 1, part_at])
                    if ring_takes(ring, way, step + 1, part_at):
                        ring_start(ring, way, step + 1, part_at)
                    if ring == 2:
                        pair_start(step + way * hx, dist, part_at)
        for array in (0, 1):
            if step < hn:
                place(array, step)
                place(array, -step)
            elif step == hn:
                place(array, step)

    def pair_dists():
        for part_at in (0, 1):
            yield 0, 0, part_at
            for step in range(1, hx + 1):
                for way in (RIGHT, LEFT):
                    if ring_takes(2, way, step, part_at):
                        yield step + way * hx, -step * SIGN[way], part_at

    for dist_at, dist, part_at in pair_dists():
        arrived(
            wts.at[part_at, weight_rows(dist, 1 - core), :],
            pair_recv.at[dist_at, part_at],
            pair_send.at[dist_at, part_at],
        )
    for copy in local[2:4]:
        copy.wait()

    def split(at):
        place_at = lax.rem(at, 2 * n) // 2
        offset = jnp.where(lax.rem(place_at, 2) == 1, (place_at + 1) // 2, lax.rem(n - place_at // 2, n))
        return at // (2 * n), offset, lax.rem(at, 2)

    r_y, r_z, r_pair = split(lax.broadcasted_iota(jnp.int32, (tokens, tokens), 0))
    c_z, c_y, c_pair = split(lax.broadcasted_iota(jnp.int32, (tokens, tokens), 1))
    same = (r_y == c_y) & (r_z == c_z) & (r_pair == c_pair)
    swap = jnp.where(same, 1.0, 0.0)
    swap_half = swap.astype(jnp.bfloat16)
    across = (((0,), (0,)), ((), ()))
    for c in range(nb):
        lanes = slice(c * BLK, (c + 1) * BLK)
        hidden = jnp.dot(picked[0, c], wts[0, :, lanes], preferred_element_type=jnp.float32)
        d_act = jnp.dot(picked[1, c], wts[1, :, lanes], preferred_element_type=jnp.float32)
        d_act = jnp.dot(swap, d_act, preferred_element_type=jnp.float32, precision=lax.Precision.HIGHEST)
        value, slope = gelu_terms(hidden)
        dh[:, lanes] = (d_act * slope).astype(jnp.bfloat16)
        act[:, lanes] = lax.dot_general(
            swap_half, value.astype(jnp.bfloat16), across, preferred_element_type=jnp.float32
        ).astype(jnp.bfloat16)

    groups = nx // 2
    group_rows = 4 * kept
    odd = lax.rem(x, 2)
    shifts = sorted(range(groups), key=lambda g: (-min(g, groups - g), g))

    def chip_of(shift, member):
        return 2 * lax.rem(x // 2 + shift, groups) + member

    def shard(chip, whose):
        return pl.ds(pl.multiple_of((2 * chip + whose) * kept, kept), kept)

    def group_compute(at):
        start = pl.multiple_of(lax.rem(x // 2 + shifts[at], groups) * group_rows, group_rows)
        for c in range(nb):
            lanes = slice(c * BLK, (c + 1) * BLK)
            for array, right in enumerate((dh, act)):
                grads[array, pl.ds(start, group_rows), lanes] = lax.dot_general(
                    picked[array, c, :, pl.ds(start, group_rows)],
                    right[:, lanes],
                    across,
                    preferred_element_type=jnp.float32,
                ).astype(jnp.bfloat16)
        for member in (0, 1):
            send(
                grads.at[:, shard(chip_of(shifts[at], member), 1 - core), :],
                sib.at[at, member],
                sib_send.at[at, member],
                sib_recv.at[at, member],
                sibling,
            )

    def group_sum(at):
        for member in (0, 1):
            arrived(sib.at[at, member], sib_recv.at[at, member], sib_send.at[at, member])
            to = lax.rem(2 * shifts[at] + member - odd + nx, nx)
            own = shard(chip_of(shifts[at], member), core)
            for array in (0, 1):
                total = grads[array, own, :].astype(jnp.float32) + sib[at, member, array].astype(jnp.float32)
                part[to, array] = total.astype(jnp.bfloat16)

    chunk = kept // ROW_PARTS

    def sum_start(way, dist, array, r):
        rows = pl.ds(r * chunk, chunk)
        send(
            part.at[dist * SIGN[way] % nx, array, rows],
            land.at[way, dist - 1, array, rows],
            sum_send.at[way, dist - 1, array, r],
            sum_recv.at[way, dist - 1, array, r],
            x_peer(SIGN[way]),
        )

    def sum_arrived(way, dist, array, r):
        rows = pl.ds(r * chunk, chunk)
        ref = land.at[way, dist - 1, array, rows]
        arrived(ref, sum_recv.at[way, dist - 1, array, r], sum_send.at[way, dist - 1, array, r])
        return land[way, dist - 1, array, r * chunk : (r + 1) * chunk].astype(jnp.float32)

    def first_hop(way, array):
        return hx if array == way else hx - 1

    group_compute(0)
    if groups > 1:
        group_compute(1)
    group_sum(0)
    for r in range(ROW_PARTS):
        for way in (RIGHT, LEFT):
            sum_start(way, hx, way, r)
    if groups > 1:
        for at in range(2, groups - 1):
            group_compute(at)
        for at in range(1, groups - 1):
            group_sum(at)
        if groups == 2:
            group_sum(1)
        for r in range(ROW_PARTS):
            for way in (RIGHT, LEFT):
                sum_start(way, hx - 1, 1 - way, r)
        if groups > 2:
            group_compute(groups - 1)
            group_sum(groups - 1)

    for dist in range(hx - 1, 0, -1):
        for which in (1, 0):
            for r in range(ROW_PARTS):
                for way in (RIGHT, LEFT):
                    array = which ^ way
                    if dist + 1 > first_hop(way, array):
                        continue
                    came = sum_arrived(way, dist + 1, array, r)
                    at, rows = dist * SIGN[way] % nx, slice(r * chunk, (r + 1) * chunk)
                    part[at, array, rows] = (part[at, array, rows].astype(jnp.float32) + came).astype(jnp.bfloat16)
                    sum_start(way, dist, array, r)

    for array in (0, 1):
        for r in range(ROW_PARTS):
            rows = slice(r * chunk, (r + 1) * chunk)
            total = part[0, array, rows].astype(jnp.float32)
            for way in (1 - array, array):
                if first_hop(way, array) >= 1:
                    total = total + sum_arrived(way, 1, array, r)
            out_ref[array, rows, :] = total.astype(jnp.bfloat16)

    for copy in sends:
        copy.wait_send()


def per_device(inputs, cotangent, w_in, w_out, keep_in, keep_out):
    nx = lax.axis_size("row") // 2
    n = math.isqrt(lax.axis_size("col"))
    features = inputs.shape[1]
    kept, width = w_in.shape
    rows = 2 * nx * kept
    nb = width // BLK
    per_tile = 2 * n // TILES
    tokens = 2 * n * n
    half = jnp.bfloat16
    hbm_spec = pl.BlockSpec(memory_space=pltpu.HBM)
    vmem_spec = pl.BlockSpec(memory_space=pltpu.VMEM)
    dma = pltpu.SemaphoreType.DMA
    top = max(nx, n) // 2
    total = pl.pallas_call(
        functools.partial(body, nx, n),
        out_shape=jax.ShapeDtypeStruct((2, kept, width), half),
        in_specs=[hbm_spec] * 6,
        out_specs=vmem_spec,
        scratch_shapes=[
            pltpu.VMEM((2, n, 2, features), half),
            pltpu.VMEM((2, TILES, per_tile, features), jnp.float32),
            [pltpu.VMEM((TILES, features // BLK, per_tile, BLK), half)] * n,
            [pltpu.VMEM((TILES, features // BLK, per_tile, BLK), half)] * n,
            pltpu.VMEM((2, rows, width), half),
            pltpu.VMEM((2, nb, tokens, rows), half),
            pltpu.VMEM((2, rows, width), half),
            pltpu.VMEM((nx // 2, 2, 2, kept, width), half),
            pltpu.VMEM((nx, 2, kept, width), half),
            pltpu.VMEM((2, nx // 2, 2, kept, width), half),
            pltpu.VMEM((tokens, width), half),
            pltpu.VMEM((tokens, width), half),
            pltpu.SMEM(keep_in.shape[::-1], jnp.int32),
            pltpu.SMEM(keep_out.shape[::-1], jnp.int32),
            dma((4, 2)),
            dma((2, n)),
            dma((2, n)),
            dma((3, 2, top, FAN)),
            dma((3, 2, top, FAN)),
            dma((nx + 1, 2)),
            dma((nx + 1, 2)),
            dma((nx // 2, 2)),
            dma((nx // 2, 2)),
            dma((2, nx // 2, 2, ROW_PARTS)),
            dma((2, nx // 2, 2, ROW_PARTS)),
        ],
        compiler_params=pltpu.CompilerParams(
            collective_id=0, has_side_effects=True, vmem_limit_bytes=48 * 1024 * 1024
        ),
        name="mlp_backward",
    )(*[pltpu.with_memory_space_constraint(v, pltpu.HBM) for v in (inputs, cotangent, w_in, w_out, keep_in.T, keep_out.T)])
    return total[0], total[1]


def solution(mesh):
    in_specs = (
        P(("row", "col"), None),
        P(("row", "col"), None),
        P("row", "col"),
        P("row", "col"),
        P(),
        P(),
    )
    out_specs = (P("row", "col"), P("row", "col"))
    return jax.shard_map(
        per_device, mesh=mesh, in_specs=in_specs, out_specs=out_specs, check_vma=False
    )
```

```python
import functools
import math

import jax
import jax.numpy as jnp
from jax import lax
from jax.experimental import pallas as pl
from jax.experimental.pallas import tpu as pltpu
from jax.sharding import PartitionSpec as P

BLK = 128
MESH = pl.DeviceIdType.MESH
RIGHT, LEFT = 0, 1
SIGN = (1, -1)
FAN = 4
TILES = 2
ROW_PARTS = 2


def gelu_terms(hidden):
    scale = math.sqrt(2.0 / math.pi)
    square = hidden * hidden
    curve = jnp.tanh(scale * (hidden + 0.044715 * (square * hidden)))
    half = 0.5 * (1.0 + curve)
    slope = half + 0.5 * hidden * (1.0 - curve * curve) * (scale * (1.0 + 3 * 0.044715 * square))
    return hidden * half, slope


def body(
    nx,
    n,
    x_hbm,
    c_hbm,
    wi_hbm,
    wo_hbm,
    keep_in_hbm,
    keep_out_hbm,
    out_ref,
    gat,
    t32,
    tok_in,
    tok_out,
    wts,
    picked,
    grads,
    sib,
    part,
    land,
    dh,
    act,
    swap,
    keep_in,
    keep_out,
    local_sem,
    p1_send,
    p1_recv,
    ring_send,
    ring_recv,
    pair_send,
    pair_recv,
    sib_send,
    sib_recv,
    sum_send,
    sum_recv,
):
    row, col = lax.axis_index("row"), lax.axis_index("col")
    x, core = row // 2, lax.rem(row, 2)
    y, z = col // n, lax.rem(col, n)
    kept, width = wi_hbm.shape
    nb = width // BLK
    tok = (tok_in, tok_out)
    _, blocks, per_tile, _ = tok_in[0].shape
    tokens = n * TILES * per_tile
    fan_blocks = blocks * TILES // FAN
    keeps = (keep_in, keep_out)
    sibling = (2 * x + 1 - core, col)
    hx, hn = nx // 2, n // 2

    def wrap(at, by, size):
        return lax.rem(at + by % size, size)

    def z_peer(d):
        return (row, y * n + wrap(z, d, n))

    def y_peer(d):
        return (row, wrap(y, d, n) * n + z)

    def x_peer(d):
        return (2 * wrap(x, d, nx) + core, col)

    peers = [z_peer(d) for d in range(1, n)] + [y_peer(d) for d in range(1, n)]
    peers += [x_peer(d) for d in sorted({1, nx - 1})] + [sibling]

    def weight_rows(dist, whose):
        start = pl.multiple_of((2 * wrap(x, dist, nx) + whose) * kept, kept)
        return pl.ds(start, kept)

    local = [
        pltpu.make_async_copy(src, gat.at[array, 0], local_sem.at[array, 0])
        for array, src in enumerate((x_hbm, c_hbm))
    ]
    local += [
        pltpu.make_async_copy(wi_hbm, wts.at[0, weight_rows(0, core), :], local_sem.at[2, 0]),
        pltpu.make_async_copy(wo_hbm, wts.at[1, weight_rows(0, core), :], local_sem.at[2, 1]),
        pltpu.make_async_copy(keep_in_hbm, keep_in, local_sem.at[3, 0]),
        pltpu.make_async_copy(keep_out_hbm, keep_out, local_sem.at[3, 1]),
    ]
    barrier = pltpu.get_barrier_semaphore()
    for peer in peers:
        pl.semaphore_signal(barrier, inc=1, device_id=peer, device_id_type=MESH)
    for copy in local:
        copy.start()
    pl.semaphore_wait(barrier, len(peers))

    sends = []

    def send(src, dst, s_sem, r_sem, device):
        copy = pltpu.make_async_remote_copy(
            src_ref=src, dst_ref=dst, send_sem=s_sem, recv_sem=r_sem, device_id=device, device_id_type=MESH
        )
        copy.start()
        sends.append(copy)

    def drain(keep):
        while len(sends) > keep:
            sends.pop(0).wait_send()

    def arrived(ref, r_sem, s_sem):
        pltpu.make_async_remote_copy(
            src_ref=ref, dst_ref=ref, send_sem=s_sem, recv_sem=r_sem, device_id=sibling, device_id_type=MESH
        ).wait_recv()

    ring_size = (n, n, nx)
    fans = (FAN, FAN, 2)
    ring_peer = (y_peer, z_peer, x_peer)

    def piece(ring, dist, part_at):
        if ring == 2:
            return wts.at[part_at, weight_rows(dist, core), :]
        tile, cut = divmod(part_at, FAN // TILES)
        return tok[ring][dist % n].at[tile, pl.ds(cut * fan_blocks, fan_blocks)]

    def ring_start(ring, way, step, part_at, src=None):
        ref = piece(ring, -(step - 1) * SIGN[way], part_at)
        send(
            ref if src is None else src,
            ref if ring == 2 else piece(ring, -step * SIGN[way], part_at),
            ring_send.at[ring, way, step - 1, part_at],
            ring_recv.at[ring, way, step - 1, part_at],
            ring_peer[ring](SIGN[way]),
        )

    def ring_takes(ring, way, step, part_at):
        top = ring_size[ring] // 2
        return step < top or (step == top and part_at * 2 // fans[ring] == way)

    def pair_start(dist_at, dist, part_at, src=None):
        ref = wts.at[part_at, weight_rows(dist, core), :]
        send(
            ref if src is None else src,
            ref,
            pair_send.at[dist_at, part_at],
            pair_recv.at[dist_at, part_at],
            sibling,
        )

    def place(array, dist):
        first = col * nb
        top = dist % n * TILES * per_tile

        def one(c, carry):
            for s in range(keep_in.shape[0]):
                block = keeps[array][s, first + c]
                for tile in range(TILES):
                    rows = slice(top + tile * per_tile, top + (tile + 1) * per_tile)
                    picked[array, c, rows, s * BLK : (s + 1) * BLK] = tok[array][dist % n][tile, block]
            return carry

        lax.fori_loop(0, nb, one, 0)

    near = sorted(range(n), key=lambda d: (min(d, n - d), d))
    for d in near[1:]:
        for array, (src, peer) in enumerate(((x_hbm, z_peer), (c_hbm, y_peer))):
            send(src, gat.at[array, d], p1_send.at[array, d], p1_recv.at[array, d], peer(n - d))
    for part_at, src in enumerate((wi_hbm, wo_hbm)):
        for way in (RIGHT, LEFT):
            if ring_takes(2, way, 1, part_at):
                ring_start(2, way, 1, part_at, src)
        pair_start(0, 0, part_at, src)

    for tile in range(TILES):
        for array in (0, 1):
            for at, d in enumerate(near[tile * n // TILES : (tile + 1) * n // TILES]):
                if d == 0:
                    local[array].wait()
                else:
                    arrived(gat.at[array, d], p1_recv.at[array, d], p1_send.at[array, d])
                t32[array, tile, 2 * at : 2 * at + 2, :] = gat[array, d].astype(jnp.float32)
            for b in range(blocks):
                tok[array][0][tile, b] = t32[array, tile, :, b * BLK : (b + 1) * BLK].astype(jnp.bfloat16)
            for part_at in range(tile * FAN // TILES, (tile + 1) * FAN // TILES):
                for way in (RIGHT, LEFT):
                    if ring_takes(array, way, 1, part_at):
                        ring_start(array, way, 1, part_at)
    for copy in local[-2:]:
        copy.wait()
    for array in (0, 1):
        place(array, 0)

    def split(at):
        place_at = lax.rem(at, 2 * n) // 2
        offset = jnp.where(lax.rem(place_at, 2) == 1, (place_at + 1) // 2, lax.rem(n - place_at // 2, n))
        return at // (2 * n), offset, lax.rem(at, 2)

    r_y, r_z, r_pair = split(lax.broadcasted_iota(jnp.int32, (tokens, tokens), 0))
    c_z, c_y, c_pair = split(lax.broadcasted_iota(jnp.int32, (tokens, tokens), 1))
    same = (r_y == c_y) & (r_z == c_z) & (r_pair == c_pair)
    swap[...] = jnp.where(same, 1.0, 0.0).astype(jnp.bfloat16)

    for step in range(1, max(hx, hn) + 1):
        for part_at in range(FAN):
            for ring in (2, 0, 1):
                for way in (RIGHT, LEFT):
                    if part_at >= fans[ring] or not ring_takes(ring, way, step, part_at):
                        continue
                    dist = -step * SIGN[way]
                    ref = piece(ring, dist, part_at)
                    arrived(ref, ring_recv.at[ring, way, step - 1, part_at], ring_send.at[ring, way, step - 1, part_at])
                    if ring_takes(ring, way, step + 1, part_at):
                        ring_start(ring, way, step + 1, part_at)
                    if ring == 2:
                        pair_start(step + way * hx, dist, part_at)
        for array in (0, 1):
            if step < hn:
                place(array, step)
                place(array, -step)
            elif step == hn:
                place(array, step)

    def pair_dists():
        for part_at in (0, 1):
            yield 0, 0, part_at
            for step in range(1, hx + 1):
                for way in (RIGHT, LEFT):
                    if ring_takes(2, way, step, part_at):
                        yield step + way * hx, -step * SIGN[way], part_at

    for dist_at, dist, part_at in pair_dists():
        arrived(
            wts.at[part_at, weight_rows(dist, 1 - core), :],
            pair_recv.at[dist_at, part_at],
            pair_send.at[dist_at, part_at],
        )
    for copy in local[2:4]:
        copy.wait()

    across = (((0,), (0,)), ((), ()))
    for c in range(nb):
        lanes = slice(c * BLK, (c + 1) * BLK)
        hidden = jnp.dot(picked[0, c], wts[0, :, lanes], preferred_element_type=jnp.float32)
        d_act = jnp.dot(picked[1, c], wts[1, :, lanes], preferred_element_type=jnp.float32)
        moved = jnp.zeros_like(d_act)
        for _ in range(3):
            head = d_act.astype(jnp.bfloat16)
            moved = moved + jnp.dot(swap[...], head, preferred_element_type=jnp.float32)
            d_act = d_act - head.astype(jnp.float32)
        d_act = moved
        value, slope = gelu_terms(hidden)
        dh[:, lanes] = (d_act * slope).astype(jnp.bfloat16)
        act[:, lanes] = lax.dot_general(
            swap[...], value.astype(jnp.bfloat16), across, preferred_element_type=jnp.float32
        ).astype(jnp.bfloat16)

    groups = nx // 2
    group_rows = 4 * kept
    odd = lax.rem(x, 2)
    shifts = sorted(range(groups), key=lambda g: (-min(g, groups - g), g))

    def chip_of(shift, member):
        return 2 * lax.rem(x // 2 + shift, groups) + member

    def shard(chip, whose):
        return pl.ds(pl.multiple_of((2 * chip + whose) * kept, kept), kept)

    def group_compute(at):
        start = pl.multiple_of(lax.rem(x // 2 + shifts[at], groups) * group_rows, group_rows)
        for c in range(nb):
            lanes = slice(c * BLK, (c + 1) * BLK)
            for array, right in enumerate((dh, act)):
                grads[array, pl.ds(start, group_rows), lanes] = lax.dot_general(
                    picked[array, c, :, pl.ds(start, group_rows)],
                    right[:, lanes],
                    across,
                    preferred_element_type=jnp.float32,
                ).astype(jnp.bfloat16)
        for member in (0, 1):
            send(
                grads.at[:, shard(chip_of(shifts[at], member), 1 - core), :],
                sib.at[at, member],
                sib_send.at[at, member],
                sib_recv.at[at, member],
                sibling,
            )

    def group_sum(at):
        for member in (0, 1):
            arrived(sib.at[at, member], sib_recv.at[at, member], sib_send.at[at, member])
            to = lax.rem(2 * shifts[at] + member - odd + nx, nx)
            own = shard(chip_of(shifts[at], member), core)
            for array in (0, 1):
                total = grads[array, own, :].astype(jnp.float32) + sib[at, member, array].astype(jnp.float32)
                part[to, array] = total.astype(jnp.bfloat16)

    chunk = kept // ROW_PARTS

    def sum_start(way, dist, array, r):
        rows = pl.ds(r * chunk, chunk)
        send(
            part.at[dist * SIGN[way] % nx, array, rows],
            land.at[way, dist - 1, array, rows],
            sum_send.at[way, dist - 1, array, r],
            sum_recv.at[way, dist - 1, array, r],
            x_peer(SIGN[way]),
        )

    def sum_arrived(way, dist, array, r):
        rows = pl.ds(r * chunk, chunk)
        ref = land.at[way, dist - 1, array, rows]
        arrived(ref, sum_recv.at[way, dist - 1, array, r], sum_send.at[way, dist - 1, array, r])
        return land[way, dist - 1, array, r * chunk : (r + 1) * chunk].astype(jnp.float32)

    def first_hop(way, array):
        return hx if array == way else hx - 1

    group_compute(0)
    if groups > 1:
        group_compute(1)
    group_sum(0)
    for r in range(ROW_PARTS):
        for way in (RIGHT, LEFT):
            sum_start(way, hx, way, r)
    if groups > 1:
        for at in range(2, groups - 1):
            group_compute(at)
        for at in range(1, groups - 1):
            group_sum(at)
        if groups == 2:
            group_sum(1)
        for r in range(ROW_PARTS):
            for way in (RIGHT, LEFT):
                sum_start(way, hx - 1, 1 - way, r)
        if groups > 2:
            group_compute(groups - 1)
            group_sum(groups - 1)

    drain(4 * ROW_PARTS)
    for dist in range(hx - 1, 0, -1):
        for which in (1, 0):
            drain(4 * ROW_PARTS)
            for r in range(ROW_PARTS):
                for way in (RIGHT, LEFT):
                    array = which ^ way
                    if dist + 1 > first_hop(way, array):
                        continue
                    came = sum_arrived(way, dist + 1, array, r)
                    at, rows = dist * SIGN[way] % nx, slice(r * chunk, (r + 1) * chunk)
                    part[at, array, rows] = (part[at, array, rows].astype(jnp.float32) + came).astype(jnp.bfloat16)
                    sum_start(way, dist, array, r)

    for array in (0, 1):
        for r in range(ROW_PARTS):
            rows = slice(r * chunk, (r + 1) * chunk)
            total = part[0, array, rows].astype(jnp.float32)
            for way in (1 - array, array):
                if first_hop(way, array) >= 1:
                    total = total + sum_arrived(way, 1, array, r)
            out_ref[array, rows, :] = total.astype(jnp.bfloat16)

    drain(0)


def per_device(inputs, cotangent, w_in, w_out, keep_in, keep_out):
    nx = lax.axis_size("row") // 2
    n = math.isqrt(lax.axis_size("col"))
    features = inputs.shape[1]
    kept, width = w_in.shape
    rows = 2 * nx * kept
    nb = width // BLK
    per_tile = 2 * n // TILES
    tokens = 2 * n * n
    half = jnp.bfloat16
    hbm_spec = pl.BlockSpec(memory_space=pltpu.HBM)
    vmem_spec = pl.BlockSpec(memory_space=pltpu.VMEM)
    dma = pltpu.SemaphoreType.DMA
    top = max(nx, n) // 2
    total = pl.pallas_call(
        functools.partial(body, nx, n),
        out_shape=jax.ShapeDtypeStruct((2, kept, width), half),
        in_specs=[hbm_spec] * 6,
        out_specs=vmem_spec,
        scratch_shapes=[
            pltpu.VMEM((2, n, 2, features), half),
            pltpu.VMEM((2, TILES, per_tile, features), jnp.float32),
            [pltpu.VMEM((TILES, features // BLK, per_tile, BLK), half)] * n,
            [pltpu.VMEM((TILES, features // BLK, per_tile, BLK), half)] * n,
            pltpu.VMEM((2, rows, width), half),
            pltpu.VMEM((2, nb, tokens, rows), half),
            pltpu.VMEM((2, rows, width), half),
            pltpu.VMEM((nx // 2, 2, 2, kept, width), half),
            pltpu.VMEM((nx, 2, kept, width), half),
            pltpu.VMEM((2, nx // 2, 2, kept, width), half),
            pltpu.VMEM((tokens, width), half),
            pltpu.VMEM((tokens, width), half),
            pltpu.VMEM((tokens, tokens), half),
            pltpu.SMEM(keep_in.shape[::-1], jnp.int32),
            pltpu.SMEM(keep_out.shape[::-1], jnp.int32),
            dma((4, 2)),
            dma((2, n)),
            dma((2, n)),
            dma((3, 2, top, FAN)),
            dma((3, 2, top, FAN)),
            dma((nx + 1, 2)),
            dma((nx + 1, 2)),
            dma((nx // 2, 2)),
            dma((nx // 2, 2)),
            dma((2, nx // 2, 2, ROW_PARTS)),
            dma((2, nx // 2, 2, ROW_PARTS)),
        ],
        compiler_params=pltpu.CompilerParams(
            collective_id=0, has_side_effects=True, vmem_limit_bytes=48 * 1024 * 1024
        ),
        name="mlp_backward",
    )(*[pltpu.with_memory_space_constraint(v, pltpu.HBM) for v in (inputs, cotangent, w_in, w_out, keep_in.T, keep_out.T)])
    return total[0], total[1]


def solution(mesh):
    in_specs = (
        P(("row", "col"), None),
        P(("row", "col"), None),
        P("row", "col"),
        P("row", "col"),
        P(),
        P(),
    )
    out_specs = (P("row", "col"), P("row", "col"))
    return jax.shard_map(
        per_device, mesh=mesh, in_specs=in_specs, out_specs=out_specs, check_vma=False
    )
```
